32 devices in a mesh: dp: 8 (over y, x, core), tensor: 4 (over z).
Axes of the slice: x: 2, y: 2, z: 4, core: 2. Of those that a mesh axis runs over, the one named last changes fastest.
Arguments:
- inputs: bfloat16 [16384, 512], P(('dp', 'tensor')), may hold values from -6 to 6
- memory: bfloat16 [4096, 512], P(('dp', 'tensor')), may hold values from -6 to 6
- prefix: int32 [16], P('dp'), may hold values from 102 to 512
- self_query: bfloat16 [512, 512], P('dp', 'tensor'), may hold values from -0.25 to 0.25
- self_query_bias: bfloat16 [512], P('tensor'), may hold values from -3 to 3
- self_key: bfloat16 [512, 512], P('dp', 'tensor'), may hold values from -0.25 to 0.25
- self_value: bfloat16 [512, 512], P('dp', 'tensor'), may hold values from -0.25 to 0.25
- self_value_bias: bfloat16 [512], P('tensor'), may hold values from -1.1953125 to 1.1953125
- self_out: bfloat16 [512, 512], P('tensor', 'dp'), may hold values from -1.5 to 1.5
- self_out_bias: bfloat16 [512], replicated, may hold values from -1.796875 to 1.796875
- self_norm_gain: bfloat16 [512], replicated, may hold values from 0.5 to 1.5
- self_norm_bias: bfloat16 [512], replicated, may hold values from -1.796875 to 1.796875
- cross_query: bfloat16 [512, 512], P('dp', 'tensor'), may hold values from -0.25 to 0.25
- cross_query_bias: bfloat16 [512], P('tensor'), may hold values from -3 to 3
- cross_key: bfloat16 [512, 512], P('dp', 'tensor'), may hold values from -0.25 to 0.25
- cross_value: bfloat16 [512, 512], P('dp', 'tensor'), may hold values from -0.25 to 0.25
- cross_value_bias: bfloat16 [512], P('tensor'), may hold values from -1.1953125 to 1.1953125
- cross_out: bfloat16 [512, 512], P('tensor', 'dp'), may hold values from -1.5 to 1.5
- cross_out_bias: bfloat16 [512], replicated, may hold values from -1.796875 to 1.796875
- cross_norm_gain: bfloat16 [512], replicated, may hold values from 0.5 to 1.5
- cross_norm_bias: bfloat16 [512], replicated, may hold values from -1.796875 to 1.796875
- feed_in: bfloat16 [512, 2048], P('dp', 'tensor'), may hold values from -0.25 to 0.25
- feed_in_bias: bfloat16 [2048], P('tensor'), may hold values from -3 to 3
- feed_out: bfloat16 [2048, 512], P('tensor', 'dp'), may hold values from -0.125 to 0.125
- feed_out_bias: bfloat16 [512], replicated, may hold values from -1.796875 to 1.796875
- feed_norm_gain: bfloat16 [512], replicated, may hold values from 0.5 to 1.5
- feed_norm_bias: bfloat16 [512], replicated, may hold values from -1.796875 to 1.796875
- cotangent: bfloat16 [16384, 512], P(('dp', 'tensor')), may hold values from -12 to 12
Outputs:
- outputs: bfloat16 [16384, 512], P(('dp', 'tensor'))
- grad_inputs: float32 [16384, 512], P(('dp', 'tensor'))
- grad_memory: float32 [4096, 512], P(('dp', 'tensor'))
- grad_self_query: float32 [512, 512], P('dp', 'tensor')
- grad_self_query_bias: float32 [512], P('tensor')
- grad_self_key: float32 [512, 512], P('dp', 'tensor')
- grad_self_value: float32 [512, 512], P('dp', 'tensor')
- grad_self_value_bias: float32 [512], P('tensor')
- grad_self_out: float32 [512, 512], P('tensor', 'dp')
- grad_self_out_bias: float32 [512], replicated
- grad_self_norm_gain: float32 [512], replicated
- grad_self_norm_bias: float32 [512], replicated
- grad_cross_query: float32 [512, 512], P('dp', 'tensor')
- grad_cross_query_bias: float32 [512], P('tensor')
- grad_cross_key: float32 [512, 512], P('dp', 'tensor')
- grad_cross_value: float32 [512, 512], P('dp', 'tensor')
- grad_cross_value_bias: float32 [512], P('tensor')
- grad_cross_out: float32 [512, 512], P('tensor', 'dp')
- grad_cross_out_bias: float32 [512], replicated
- grad_cross_norm_gain: float32 [512], replicated
- grad_cross_norm_bias: float32 [512], replicated
- grad_feed_in: float32 [512, 2048], P('dp', 'tensor')
- grad_feed_in_bias: float32 [2048], P('tensor')
- grad_feed_out: float32 [2048, 512], P('tensor', 'dp')
- grad_feed_out_bias: float32 [512], replicated
- grad_feed_norm_gain: float32 [512], replicated
- grad_feed_norm_bias: float32 [512], replicated
The draws below stay inside these ranges and needn't reach their ends.
All inputs are finite; a program needn't handle non-finite values.
Results may differ from the reference program's by a relative error of at most 0.025.
Values may be sent and summed in bfloat16 or wider, within the bound.
No kernel may reach another device: no remote copies, remote signals or barrier semaphores. Data moves between devices by JAX's collectives and lax.ppermute only.
A program may use at most 128 MiB of HBM per device.

```python
import jax
import jax.numpy as jnp
from jax import lax

D = 512
FF = 2048
HEADS = 8
HD = 64
LEN = 1024
MEM = 256
SEQS = 16
TOKENS = 16384
MEM_ROWS = 4096


def draw_cotangent(key, part):
    row_pos = jnp.arange(TOKENS, dtype=jnp.float32)[:, None] / max(TOKENS - 1, 1)
    row_scale = 1.0 + 2.0 * row_pos
    base_draw = jax.random.normal(key, (TOKENS, D), jnp.float32)
    return jnp.clip(base_draw * row_scale, -12.0, 12.0).astype(jnp.bfloat16)


def with_ends(array, rng, least, top_value):
    longest = array.shape.index(max(array.shape))
    spots = []
    for shift in (0, 1):
        where = [jax.random.randint(jax.random.fold_in(rng, axis), (), 0, length) for axis, length in enumerate(array.shape)]
        where[longest] = (where[longest] + shift) % array.shape[longest]
        spots.append(tuple(where))
    return array.at[spots[0]].set(least).at[spots[1]].set(top_value)


def levels(key, extent, pieces, least, top_value):
    def one(position, parts):
        heights = jax.random.uniform(jax.random.fold_in(jax.random.fold_in(key, 6), position), (parts,), jnp.float32, least / len(pieces), top_value / len(pieces))
        return jnp.repeat(jnp.exp(heights), extent[position] // parts).reshape((-1,) + (1,) * (len(extent) - position - 1))

    gain = one(*pieces[0])
    for cut in pieces[1:]:
        gain = gain * one(*cut)
    return gain


def gaussian(stream_key, shape, spread, bound, cuts=(), held_as=jnp.bfloat16):
    values = spread * jax.random.normal(stream_key, shape, jnp.float32)
    if cuts:
        values = values * levels(stream_key, shape, cuts, -0.22, 0.18)
    return jnp.clip(values, -bound, bound).astype(held_as)


def setup_inputs(seed: int = 0) -> dict:
    key_of = jax.random.split(jax.random.key(seed), 29)
    inputs = gaussian(key_of[0], (TOKENS, D), 1.0, 6.0, ((0, 32),))
    memory = gaussian(key_of[1], (MEM_ROWS, D), 1.0, 6.0, ((0, 32),))
    prefix = with_ends(jax.random.randint(key_of[2], (SEQS,), LEN // 10, LEN // 2 + 1), jax.random.fold_in(key_of[2], 1), LEN // 10, (LEN // 2 + 1) - 1).astype(jnp.int32)
    self_query = gaussian(key_of[3], (D, D), D ** -0.5, 0.25, ((0, 8), (1, 4)))
    self_query_bias = gaussian(key_of[4], (D,), 0.5, 3.0, ((0, 4),))
    self_key = gaussian(key_of[5], (D, D), D ** -0.5, 0.25, ((0, 8), (1, 4)))
    self_value = gaussian(key_of[6], (D, D), D ** -0.5, 0.25, ((0, 8), (1, 4)))
    self_value_bias = gaussian(key_of[7], (D,), 0.2, 1.1953125, ((0, 4),))
    self_out = gaussian(key_of[8], (D, D), (D // 32) ** -0.5, 1.5, ((0, 4), (1, 8)))
    self_out_bias = gaussian(key_of[9], (D,), 0.3, 1.796875)
    self_norm_gain = jnp.clip(1.0 + 0.1 * jax.random.normal(key_of[10], (D,), jnp.float32), 0.5, 1.5).astype(jnp.bfloat16)
    self_norm_bias = gaussian(key_of[11], (D,), 0.3, 1.796875)
    cross_query = gaussian(key_of[12], (D, D), D ** -0.5, 0.25, ((0, 8), (1, 4)))
    cross_query_bias = gaussian(key_of[13], (D,), 0.5, 3.0, ((0, 4),))
    cross_key = gaussian(key_of[14], (D, D), D ** -0.5, 0.25, ((0, 8), (1, 4)))
    cross_value = gaussian(key_of[15], (D, D), D ** -0.5, 0.25, ((0, 8), (1, 4)))
    cross_value_bias = gaussian(key_of[16], (D,), 0.2, 1.1953125, ((0, 4),))
    cross_out = gaussian(key_of[17], (D, D), (D // 32) ** -0.5, 1.5, ((0, 4), (1, 8)))
    cross_out_bias = gaussian(key_of[18], (D,), 0.3, 1.796875)
    cross_norm_gain = jnp.clip(1.0 + 0.1 * jax.random.normal(key_of[19], (D,), jnp.float32), 0.5, 1.5).astype(jnp.bfloat16)
    cross_norm_bias = gaussian(key_of[20], (D,), 0.3, 1.796875)
    feed_in = gaussian(key_of[21], (D, FF), D ** -0.5, 0.25, ((0, 8), (1, 4)))
    feed_in_bias = gaussian(key_of[22], (FF,), 0.5, 3.0, ((0, 4),))
    feed_out = gaussian(key_of[23], (FF, D), FF ** -0.5, 0.125, ((0, 4), (1, 8)))
    feed_out_bias = gaussian(key_of[24], (D,), 0.3, 1.796875)
    feed_norm_gain = jnp.clip(1.0 + 0.1 * jax.random.normal(key_of[25], (D,), jnp.float32), 0.5, 1.5).astype(jnp.bfloat16)
    feed_norm_bias = gaussian(key_of[26], (D,), 0.3, 1.796875)
    cotangent = draw_cotangent(jax.random.fold_in(key_of[28], 71), 0)
    return {"inputs": inputs, "memory": memory, "prefix": prefix, "self_query": self_query, "self_query_bias": self_query_bias, "self_key": self_key, "self_value": self_value, "self_value_bias": self_value_bias, "self_out": self_out, "self_out_bias": self_out_bias, "self_norm_gain": self_norm_gain, "self_norm_bias": self_norm_bias, "cross_query": cross_query, "cross_query_bias": cross_query_bias, "cross_key": cross_key, "cross_value": cross_value, "cross_value_bias": cross_value_bias, "cross_out": cross_out, "cross_out_bias": cross_out_bias, "cross_norm_gain": cross_norm_gain, "cross_norm_bias": cross_norm_bias, "feed_in": feed_in, "feed_in_bias": feed_in_bias, "feed_out": feed_out, "feed_out_bias": feed_out_bias, "feed_norm_gain": feed_norm_gain, "feed_norm_bias": feed_norm_bias, "cotangent": cotangent}


@jax.custom_vjp
def low(v):
    return lax.optimization_barrier(v.astype(jnp.bfloat16)).astype(jnp.float32)

@jax.custom_vjp
def low_back(v):
    return v

def low_keep(v):
    return (low(v), None)

def low_pass(kept, grad):
    return (grad,)

def back_keep(v):
    return (v, None)

def back_low(kept, grad):
    return (low(grad),)
low.defvjp(low_keep, low_pass)
low_back.defvjp(back_keep, back_low)

def matmul_high(left_side, right_side):
    return jnp.dot(left_side, right_side, precision=lax.Precision.HIGHEST)

def rounded(values):
    return low(low_back(values))

def layer_norm(summed, norm_gain, norm_shift):
    row_mean = lax.optimization_barrier(jnp.mean(summed, axis=-1, keepdims=True))
    centred = summed - row_mean
    variance = lax.optimization_barrier(jnp.mean(centred * centred, axis=-1, keepdims=True))
    return centred * lax.rsqrt(variance + 1e-05) * norm_gain + norm_shift

def attend(query_heads, key_heads, value_heads, allowed):
    scores = jnp.einsum('qhd,khd->hqk', query_heads, key_heads, precision=lax.Precision.HIGHEST) * HD ** (-0.5)
    scores = jnp.where(allowed[None], low_back(scores), -1e+30)
    row_peak = lax.optimization_barrier(jnp.max(scores, axis=-1, keepdims=True))
    exponent = jnp.exp(scores - row_peak)
    weights_soft = exponent / lax.optimization_barrier(jnp.sum(exponent, axis=-1, keepdims=True))
    return jnp.einsum('hqk,khd->qhd', low(weights_soft), value_heads, precision=lax.Precision.HIGHEST)

def self_attention(queries, keys, values, prefix):
    positions = jnp.arange(LEN, dtype=jnp.int32)
    causal = positions[None, :] <= positions[:, None]
    head_shape = (SEQS, LEN, HEADS, HD)

    def one_sequence(seq_items):
        query_seq, key_seq, value_seq, prefix_len = seq_items
        allowed = causal | (positions[None, :] < prefix_len)
        return attend(query_seq, key_seq, value_seq, allowed)
    mapped = lax.map(jax.checkpoint(one_sequence), (queries.reshape(head_shape), keys.reshape(head_shape), values.reshape(head_shape), prefix))
    return mapped.reshape(TOKENS, D)

def cross_attention(queries, keys, values):
    allowed = jnp.ones((LEN, MEM), dtype=jnp.bool_)

    def one_sequence(seq_items):
        query_seq, key_seq, value_seq = seq_items
        return attend(query_seq, key_seq, value_seq, allowed)
    mapped = lax.map(jax.checkpoint(one_sequence), (queries.reshape(SEQS, LEN, HEADS, HD), keys.reshape(SEQS, MEM, HEADS, HD), values.reshape(SEQS, MEM, HEADS, HD)))
    return mapped.reshape(TOKENS, D)

def forward(inputs, memory, weights, prefix):
    self_query, self_query_bias, self_key, self_value, self_value_bias, self_out, self_out_bias, self_norm_gain, self_norm_bias, cross_query, cross_query_bias, cross_key, cross_value, cross_value_bias, cross_out, cross_out_bias, cross_norm_gain, cross_norm_bias, feed_in, feed_in_bias, feed_out, feed_out_bias, feed_norm_gain, feed_norm_bias = weights
    query_one = rounded(matmul_high(inputs, self_query) + self_query_bias)
    key_one = rounded(matmul_high(inputs, self_key))
    value_one = rounded(matmul_high(inputs, self_value) + self_value_bias)
    context_one = rounded(self_attention(query_one, key_one, value_one, prefix))
    branch_one = low_back(matmul_high(context_one, self_out) + self_out_bias)
    first_out = layer_norm(inputs + branch_one, self_norm_gain, self_norm_bias)
    first_low = low(first_out)
    query_two = rounded(matmul_high(first_low, cross_query) + cross_query_bias)
    key_two = rounded(matmul_high(memory, cross_key))
    value_two = rounded(matmul_high(memory, cross_value) + cross_value_bias)
    context_two = rounded(cross_attention(query_two, key_two, value_two))
    branch_two = low_back(matmul_high(context_two, cross_out) + cross_out_bias)
    second_out = layer_norm(first_out + branch_two, cross_norm_gain, cross_norm_bias)
    second_low = low(second_out)
    hidden = low_back(matmul_high(second_low, feed_in) + feed_in_bias)
    active = low(jax.nn.silu(hidden))
    branch_three = low_back(matmul_high(active, feed_out) + feed_out_bias)
    return layer_norm(second_out + branch_three, feed_norm_gain, feed_norm_bias)

def reference(inputs, memory, prefix, self_query, self_query_bias, self_key, self_value, self_value_bias, self_out, self_out_bias, self_norm_gain, self_norm_bias, cross_query, cross_query_bias, cross_key, cross_value, cross_value_bias, cross_out, cross_out_bias, cross_norm_gain, cross_norm_bias, feed_in, feed_in_bias, feed_out, feed_out_bias, feed_norm_gain, feed_norm_bias, cotangent):
    weights = (self_query, self_query_bias, self_key, self_value, self_value_bias, self_out, self_out_bias, self_norm_gain, self_norm_bias, cross_query, cross_query_bias, cross_key, cross_value, cross_value_bias, cross_out, cross_out_bias, cross_norm_gain, cross_norm_bias, feed_in, feed_in_bias, feed_out, feed_out_bias, feed_norm_gain, feed_norm_bias)
    weights_float = tuple((weight.astype(jnp.float32) for weight in weights))

    def run_layer(tokens_float, memory_float, params_float):
        return forward(tokens_float, memory_float, params_float, prefix)
    result, pullback = jax.vjp(run_layer, inputs.astype(jnp.float32), memory.astype(jnp.float32), weights_float)
    grad_inputs, grad_memory, grad_weights = pullback(cotangent.astype(jnp.float32))
    grad_self_query, grad_self_query_bias, grad_self_key, grad_self_value, grad_self_value_bias, grad_self_out, grad_self_out_bias, grad_self_norm_gain, grad_self_norm_bias, grad_cross_query, grad_cross_query_bias, grad_cross_key, grad_cross_value, grad_cross_value_bias, grad_cross_out, grad_cross_out_bias, grad_cross_norm_gain, grad_cross_norm_bias, grad_feed_in, grad_feed_in_bias, grad_feed_out, grad_feed_out_bias, grad_feed_norm_gain, grad_feed_norm_bias = grad_weights
    return (result.astype(jnp.bfloat16), grad_inputs, grad_memory, grad_self_query, grad_self_query_bias, grad_self_key, grad_self_value, grad_self_value_bias, grad_self_out, grad_self_out_bias, grad_self_norm_gain, grad_self_norm_bias, grad_cross_query, grad_cross_query_bias, grad_cross_key, grad_cross_value, grad_cross_value_bias, grad_cross_out, grad_cross_out_bias, grad_cross_norm_gain, grad_cross_norm_bias, grad_feed_in, grad_feed_in_bias, grad_feed_out, grad_feed_out_bias, grad_feed_norm_gain, grad_feed_norm_bias)
```

```python
import functools

import jax
import jax.numpy as jnp
from jax import lax
from jax.experimental import pallas as pl
from jax.experimental.pallas import tpu as pltpu
from jax.sharding import PartitionSpec as P

HD = 64
LEN = 1024
MEM = 256
LANES = 128
EPSILON = 1e-05
MASKED = -1e30
SCALE = float(HD) ** (-0.5)
HALF = 256

bf16 = jnp.bfloat16
f32 = jnp.float32
VM = pltpu.VMEM


def nn(a, b):
    return lax.dot_general(a, b, (((1,), (0,)), ((), ())), preferred_element_type=f32)


def nt(a, b):
    return lax.dot_general(a, b, (((1,), (1,)), ((), ())), preferred_element_type=f32)


def tn(a, b):
    return lax.dot_general(a, b, (((0,), (0,)), ((), ())), preferred_element_type=f32)


def norm_forward(summed):
    row_mean = jnp.mean(summed, axis=-1, keepdims=True)
    centred = summed - row_mean
    variance = jnp.mean(centred * centred, axis=-1, keepdims=True)
    inverse = lax.rsqrt(variance + EPSILON)
    return centred * inverse, inverse


def norm_backward(grad_out, normed, inverse, gain):
    grad_normed = grad_out * gain
    return inverse * (
        grad_normed
        - jnp.mean(grad_normed, axis=-1, keepdims=True)
        - normed * jnp.mean(grad_normed * normed, axis=-1, keepdims=True)
    )


def column_sum(array):
    return jnp.sum(array, axis=0, keepdims=True)


def first_head(shape):
    return lax.broadcasted_iota(jnp.int32, shape, 1) < HD


def self_forward_kernel(
    info, x_own, x_oth, wq, wk, wv, bq, bv,
    q_out, ko_out, kt_out, vo_out, vt_out, eo_out, et_out, ctx_out, linv_out,
):
    prefix = info[0]
    odd = info[1]
    own = x_own[...]
    query = (nn(own, wq[...]) + bq[...]).astype(bf16)
    key_own = nn(own, wk[...]).astype(bf16)
    value_own = (nn(own, wv[...]) + bv[...]).astype(bf16)
    q_out[...] = query
    ko_out[...] = key_own
    vo_out[...] = value_own
    scaled = query * jnp.asarray(SCALE, bf16)
    rows = own.shape[0]

    def block(number, own_keys, with_other):
        low = number * HALF
        high = low + HALF
        lane = first_head((HALF, LANES))
        part = scaled[low:high]
        contexts = []
        inverses = []
        for head in range(2):
            mine = lane if head == 0 else ~lane
            masked_query = jnp.where(mine, part, jnp.zeros_like(part))
            s_own = nt(masked_query, ko_out[:own_keys, :])
            row = low + lax.broadcasted_iota(jnp.int32, s_own.shape, 0)
            col = lax.broadcasted_iota(jnp.int32, s_own.shape, 1)
            s_own = jnp.where((col <= row) | (col < prefix), s_own, MASKED)
            peak = jnp.max(s_own, axis=-1, keepdims=True)
            if with_other:
                s_oth = nt(masked_query, kt_out[...])
                peak = jnp.maximum(peak, jnp.max(s_oth, axis=-1, keepdims=True))
            e_own = jnp.exp(s_own - peak)
            total = jnp.sum(e_own, axis=-1, keepdims=True)
            e_own = e_own.astype(bf16)
            eo_out[head, low:high, :own_keys] = e_own
            context = nn(e_own, vo_out[:own_keys, :])
            if with_other:
                e_oth = jnp.exp(s_oth - peak)
                total = total + jnp.sum(e_oth, axis=-1, keepdims=True)
                e_oth = e_oth.astype(bf16)
                et_out[head, low:high, :] = e_oth
                context = context + nn(e_oth, vt_out[...])
            inverse = 1.0 / total
            contexts.append(context * inverse)
            inverses.append(inverse)
        ctx_out[low:high, :] = jnp.where(lane, contexts[0], contexts[1]).astype(bf16)
        linv_out[0, low:high, :] = jnp.where(lane, inverses[0], inverses[1])

    @pl.when(odd == 1)
    def _():
        other = x_oth[...]
        kt_out[...] = nn(other, wk[...]).astype(bf16)
        vt_out[...] = (nn(other, wv[...]) + bv[...]).astype(bf16)
        for number in range(rows // HALF):
            block(number, (number + 1) * HALF, True)

    @pl.when(odd == 0)
    def _():
        for number in range(rows // HALF):
            block(number, rows, False)


def cross_forward_kernel(
    x_own, ctx_one, wo, bo, g1, s1, wcq, bcq, mem_own, mem_oth, wck, wcv, bcv, wco, bco,
    n1_out, inv1_out, first_out, q_out, k_out, v_out, e_out, ctx_out, linv_out, n2_out, inv2_out,
):
    summed = x_own[...].astype(f32) + nt(ctx_one[...], wo[...]) + bo[...]
    normed, inverse = norm_forward(summed)
    n1_out[...] = normed
    inv1_out[...] = jnp.broadcast_to(inverse, inv1_out.shape)
    first = normed * g1[...] + s1[...]
    first_low = first.astype(bf16)
    first_out[...] = first_low
    q_out[...] = (nn(first_low, wcq[...]) + bcq[...]).astype(bf16)
    half = mem_own.shape[0]
    k_out[:half, :] = nn(mem_own[...], wck[...]).astype(bf16)
    k_out[half:, :] = nn(mem_oth[...], wck[...]).astype(bf16)
    v_out[:half, :] = (nn(mem_own[...], wcv[...]) + bcv[...]).astype(bf16)
    v_out[half:, :] = (nn(mem_oth[...], wcv[...]) + bcv[...]).astype(bf16)
    rows = x_own.shape[0]

    def pair(number, carry):
        start = pl.multiple_of(number * LANES, LANES)
        columns = pl.ds(start, LANES)
        lane = first_head((rows, LANES))
        part = q_out[:, columns] * jnp.asarray(SCALE, bf16)
        keys = k_out[:, columns]
        values = v_out[:, columns]
        contexts = []
        inverses = []
        for head in range(2):
            mine = lane if head == 0 else ~lane
            scores = nt(jnp.where(mine, part, jnp.zeros_like(part)), keys)
            peak = jnp.max(scores, axis=-1, keepdims=True)
            weights = jnp.exp(scores - peak)
            inverse = 1.0 / jnp.sum(weights, axis=-1, keepdims=True)
            weights = weights.astype(bf16)
            e_out[2 * number + head] = weights
            contexts.append(nn(weights, values) * inverse)
            inverses.append(inverse)
        ctx_out[:, columns] = jnp.where(lane, contexts[0], contexts[1]).astype(bf16)
        linv_out[number] = jnp.where(lane, inverses[0], inverses[1])
        return carry

    lax.fori_loop(0, x_own.shape[1] // LANES, pair, 0)
    summed = first + nt(ctx_out[...], wco[...]) + bco[...]
    normed, inverse = norm_forward(summed)
    n2_out[...] = normed
    inv2_out[...] = jnp.broadcast_to(inverse, inv2_out.shape)


def feed_kernel(
    n2, inv2, g2, s2, win, bin_, wout, bout, g3, s3, cotangent,
    out_ref, gout_ref, gin_ref, du2_ref, vec_ref, vech_ref,
    hidden_ref, active_ref, dhid_ref,
):
    normed_two = n2[...]
    gain_two = g2[...]
    second = normed_two * gain_two + s2[...]
    second_low = second.astype(bf16)
    width = win.shape[1]
    step = 512
    branch = second + bout[...]
    for start in range(0, width, step):
        columns = slice(start, start + step)
        hidden = nn(second_low, win[:, columns]) + bin_[:, columns]
        hidden_ref[:, columns] = hidden
        active = (hidden / (1.0 + jnp.exp(-hidden))).astype(bf16)
        active_ref[:, columns] = active
        branch = branch + nt(active, wout[:, columns])
    normed, inverse = norm_forward(branch)
    gain = g3[...]
    out_ref[...] = (normed * gain + s3[...]).astype(bf16)
    grad = cotangent[...].astype(f32)
    vec_ref[0:1, :] = column_sum(grad * normed)
    vec_ref[1:2, :] = column_sum(grad)
    du3 = norm_backward(grad, normed, inverse, gain)
    dbranch = du3.astype(bf16)
    vec_ref[2:3, :] = column_sum(dbranch.astype(f32))
    dsecond = du3
    for start in range(0, width, step):
        columns = slice(start, start + step)
        gout_ref[:, columns] = tn(dbranch, active_ref[:, columns]).astype(bf16)
        dactive = nn(dbranch, wout[:, columns])
        hidden = hidden_ref[:, columns]
        sig = 1.0 / (1.0 + jnp.exp(-hidden))
        dhidden = (dactive * sig * (1.0 + hidden * (1.0 - sig))).astype(bf16)
        vech_ref[:, columns] = column_sum(dhidden.astype(f32))
        gin_ref[:, columns] = tn(second_low, dhidden).astype(bf16)
        dsecond = dsecond + nt(dhidden, win[:, columns])
    vec_ref[3:4, :] = column_sum(dsecond * normed_two)
    vec_ref[4:5, :] = column_sum(dsecond)
    du2 = norm_backward(dsecond, normed_two, inv2[:, :1], gain_two)
    du2_ref[...] = du2
    vec_ref[5:6, :] = column_sum(du2.astype(bf16).astype(f32))
    vec_ref[6:8, :] = jnp.zeros_like(vec_ref[6:8, :])


def cross_backward_kernel(
    du2, wco, ctx_two, q, k, v, e, linv, first_low, mem_own, mem_oth, wcq, wck, wcv,
    n1, inv1, g1, wo, ctx_one,
    gco_ref, gcq_ref, gck_ref, gcv_ref, gmo_ref, gmt_ref, du1_ref, dctx_ref, go_ref, vec_ref,
    dcon_ref, dq_ref, dk_ref, dv_ref,
):
    dbranch = du2[...].astype(bf16)
    dcon_ref[...] = nn(dbranch, wco[...]).astype(bf16)
    gco_ref[...] = tn(dbranch, ctx_two[...]).astype(bf16)
    rows = du2.shape[0]
    keys_count = k.shape[0]

    def pair(number, carry):
        start = pl.multiple_of(number * LANES, LANES)
        columns = pl.ds(start, LANES)
        lane = first_head((rows, LANES))
        lane_k = first_head((keys_count, LANES))
        grad = dcon_ref[:, columns].astype(f32) * linv[number]
        grad_low = grad.astype(bf16)
        weighted = grad * ctx_two[:, columns].astype(f32)
        keys = k[:, columns]
        values = v[:, columns]
        queries = q[:, columns]
        dqs, dks, dvs = [], [], []
        for head in range(2):
            mine = lane if head == 0 else ~lane
            delta = jnp.sum(jnp.where(mine, weighted, 0.0), axis=-1, keepdims=True)
            dweights = nt(jnp.where(mine, grad_low, jnp.zeros_like(grad_low)), values)
            weights = e[2 * number + head]
            dscores = (weights.astype(f32) * (dweights - delta)).astype(bf16)
            dqs.append(nn(dscores, keys))
            dks.append(tn(dscores, queries))
            dvs.append(tn(weights, grad_low))
        dq_ref[:, columns] = (jnp.where(lane, dqs[0], dqs[1]) * SCALE).astype(bf16)
        dk_ref[:, columns] = (jnp.where(lane_k, dks[0], dks[1]) * SCALE).astype(bf16)
        dv_ref[:, columns] = jnp.where(lane_k, dvs[0], dvs[1]).astype(bf16)
        return carry

    lax.fori_loop(0, du2.shape[1] // LANES, pair, 0)
    dq = dq_ref[...]
    half = mem_own.shape[0]
    vec_ref[0:1, :] = column_sum(dq.astype(f32))
    vec_ref[1:2, :] = column_sum(dv_ref[...].astype(f32))
    gcq_ref[...] = tn(first_low[...], dq).astype(bf16)
    dk_own = dk_ref[:half, :]
    dk_oth = dk_ref[half:, :]
    dv_own = dv_ref[:half, :]
    dv_oth = dv_ref[half:, :]
    gck_ref[...] = (tn(mem_own[...], dk_own) + tn(mem_oth[...], dk_oth)).astype(bf16)
    gcv_ref[...] = (tn(mem_own[...], dv_own) + tn(mem_oth[...], dv_oth)).astype(bf16)
    gmo_ref[...] = nt(dk_own, wck[...]) + nt(dv_own, wcv[...])
    gmt_ref[...] = (nt(dk_oth, wck[...]) + nt(dv_oth, wcv[...])).astype(bf16)
    dfirst = du2[...] + nt(dq, wcq[...])
    normed = n1[...]
    vec_ref[2:3, :] = column_sum(dfirst * normed)
    vec_ref[3:4, :] = column_sum(dfirst)
    du1 = norm_backward(dfirst, normed, inv1[:, :1], g1[...])
    du1_ref[...] = du1
    dbranch_one = du1.astype(bf16)
    vec_ref[4:5, :] = column_sum(dbranch_one.astype(f32))
    vec_ref[5:8, :] = jnp.zeros_like(vec_ref[5:8, :])
    dctx_ref[...] = nn(dbranch_one, wo[...]).astype(bf16)
    go_ref[...] = tn(dbranch_one, ctx_one[...]).astype(bf16)


def self_backward_kernel(
    info, q, ko, kt, vo, vt, eo, et, ctx, linv, dctx,
    dq_ref, dko_ref, dkt_ref, dvo_ref, dvt_ref,
):
    odd = info[1]
    rows = q.shape[0]
    queries = q[...]
    grad = dctx[...].astype(f32) * linv[0]
    grad_low = grad.astype(bf16)
    weighted = grad * ctx[...].astype(f32)
    lane = first_head((rows, LANES))

    def run(with_other):
        outs = []
        for head in range(2):
            mine = lane if head == 0 else ~lane
            delta = jnp.sum(jnp.where(mine, weighted, 0.0), axis=-1, keepdims=True)
            grad_mine = jnp.where(mine, grad_low, jnp.zeros_like(grad_low))
            if with_other:
                top = HALF
                w_top = eo[head, :top, :top]
                w_low = eo[head, top:, :]
                d_top = nt(grad_mine[:top], vo[:top, :])
                d_low = nt(grad_mine[top:], vo[...])
                s_top = (w_top.astype(f32) * (d_top - delta[:top])).astype(bf16)
                s_low = (w_low.astype(f32) * (d_low - delta[top:])).astype(bf16)
                dq = jnp.concatenate([nn(s_top, ko[:top, :]), nn(s_low, ko[...])], axis=0)
                dk_a = tn(s_low, queries[top:])
                dv_a = tn(w_low, grad_low[top:])
                dk_b = tn(s_top, queries[:top])
                dv_b = tn(w_top, grad_low[:top])
                dk = jnp.concatenate([dk_a[:top] + dk_b, dk_a[top:]], axis=0)
                dv = jnp.concatenate([dv_a[:top] + dv_b, dv_a[top:]], axis=0)
                weights = et[head]
                dweights = nt(grad_mine, vt[...])
                dscores = (weights.astype(f32) * (dweights - delta)).astype(bf16)
                dq = dq + nn(dscores, kt[...])
                outs.append((dq, dk, dv, tn(dscores, queries), tn(weights, grad_low)))
            else:
                weights = eo[head]
                dweights = nt(grad_mine, vo[...])
                dscores = (weights.astype(f32) * (dweights - delta)).astype(bf16)
                outs.append(
                    (nn(dscores, ko[...]), tn(dscores, queries), tn(weights, grad_low))
                )
        joined = [jnp.where(lane, a, b) for a, b in zip(*outs)]
        dq_ref[...] = (joined[0] * SCALE).astype(bf16)
        dko_ref[...] = (joined[1] * SCALE).astype(bf16)
        dvo_ref[...] = joined[2].astype(bf16)
        if with_other:
            dkt_ref[...] = (joined[3] * SCALE).astype(bf16)
            dvt_ref[...] = joined[4].astype(bf16)
        else:
            dkt_ref[...] = jnp.zeros_like(dkt_ref)
            dvt_ref[...] = jnp.zeros_like(dvt_ref)

    @pl.when(odd == 1)
    def _():
        run(True)

    @pl.when(odd == 0)
    def _():
        run(False)


def self_weights_kernel(
    x_own, x_oth, dq, dko, dkt, dvo, dvt, wq, wk, wv, du1,
    gq_ref, gk_ref, gv_ref, gio_ref, git_ref, vec_ref,
):
    own = x_own[...]
    oth = x_oth[...]
    gq_ref[...] = tn(own, dq[...]).astype(bf16)
    gk_ref[...] = (tn(own, dko[...]) + tn(oth, dkt[...])).astype(bf16)
    gv_ref[...] = (tn(own, dvo[...]) + tn(oth, dvt[...])).astype(bf16)
    git_ref[...] = (nt(dkt[...], wk[...]) + nt(dvt[...], wv[...])).astype(bf16)
    gio_ref[...] = (
        du1[...] + nt(dq[...], wq[...]) + nt(dko[...], wk[...]) + nt(dvo[...], wv[...])
    )
    vec_ref[0:1, :] = column_sum(dq[...].astype(f32))
    vec_ref[1:2, :] = column_sum(dvo[...].astype(f32)) + column_sum(dvt[...].astype(f32))
    vec_ref[2:8, :] = jnp.zeros_like(vec_ref[2:8, :])


def shape(dims, dtype=bf16):
    return jax.ShapeDtypeStruct(dims, dtype)


def whole_call(kernel, name, outs, args, flops, scratch=()):
    spec = pl.BlockSpec(memory_space=VM)
    return pl.pallas_call(
        kernel,
        name=name,
        out_shape=tuple(outs),
        in_specs=[spec] * len(args),
        out_specs=tuple([spec] * len(outs)),
        scratch_shapes=list(scratch),
        compiler_params=pltpu.CompilerParams(vmem_limit_bytes=60 * 2**20),
        cost_estimate=pl.CostEstimate(flops=flops, transcendentals=0, bytes_accessed=8 * 2**20),
    )(*args)


def swap(array, axis, mask):
    count = lax.axis_size(axis)
    return lax.ppermute(array, axis, [(i, i ^ mask) for i in range(count)])


def gather_stages(block):
    along_z = [block] + [swap(block, "tensor", r) for r in range(1, lax.axis_size("tensor"))]
    column = jnp.stack(along_z)
    chips = lax.axis_size("dp") // 2
    across = [column] + [swap(column, "dp", a << 1) for a in range(1, chips)]
    plane = jnp.stack(across)
    return plane, swap(plane, "dp", 1)


def place_info():
    return jnp.stack([lax.axis_index("dp"), lax.axis_index("tensor")]).astype(jnp.int32)


def join_kernel(count, chips, depth, info, plane, other, *outs):
    me = info[0]
    z = info[1]
    rows, width = plane.shape[2] // count, plane.shape[3]
    for core, ref in enumerate((plane, other)):
        for chip in range(chips):
            for r in range(depth):
                row = pl.multiple_of((me ^ (chip << 1 | core)) * rows, rows)
                col = pl.multiple_of((z ^ r) * width, LANES)
                for number, out in enumerate(outs):
                    out[pl.ds(row, rows), pl.ds(col, width)] = ref[
                        chip, r, number * rows : (number + 1) * rows, :
                    ]


def gather_weights(blocks):
    rows, width = blocks[0].shape
    count = len(blocks)
    plane, other = gather_stages(jnp.concatenate(blocks, axis=0))
    chips, depth = plane.shape[:2]
    full = (rows * chips * 2, width * depth)
    if width % LANES == 0 and rows % 16 == 0:
        spec = pl.BlockSpec(memory_space=VM)
        return pl.pallas_call(
            functools.partial(join_kernel, count, chips, depth),
            name="join_weights",
            out_shape=tuple([shape(full)] * count),
            in_specs=[pl.BlockSpec(memory_space=pltpu.SMEM), spec, spec],
            out_specs=tuple([spec] * count),
        )(place_info(), plane, other)
    pieces = jnp.stack([plane, other], axis=1).reshape(chips * 2, depth, count, rows, width)
    pieces = jnp.take(pieces, lax.axis_index("dp") ^ jnp.arange(chips * 2), axis=0)
    pieces = jnp.take(pieces, lax.axis_index("tensor") ^ jnp.arange(depth), axis=1)
    whole = pieces.transpose(2, 0, 3, 1, 4).reshape((count,) + full)
    return tuple(whole[i] for i in range(count))


def split_kernel(count, chips, depth, info, *refs):
    me = info[0]
    z = info[1]
    grads = refs[:count]
    keep, send = refs[count:]
    rows, width = keep.shape[2] // count, keep.shape[3]
    for core, ref in enumerate((keep, send)):
        for chip in range(chips):
            for r in range(depth):
                row = pl.multiple_of((me ^ (chip << 1 | core)) * rows, rows)
                col = pl.multiple_of((z ^ r) * width, LANES)
                for number, grad in enumerate(grads):
                    ref[chip, r, number * rows : (number + 1) * rows, :] = grad[
                        pl.ds(row, rows), pl.ds(col, width)
                    ]


def add_low(*terms):
    total = terms[0].astype(f32)
    for term in terms[1:]:
        total = total + term.astype(f32)
    return total


def scatter_weights(grads):
    count = len(grads)
    chips = lax.axis_size("dp") // 2
    depth = lax.axis_size("tensor")
    rows, width = grads[0].shape[0] // (2 * chips), grads[0].shape[1] // depth
    if width % LANES == 0 and rows % 16 == 0:
        spec = pl.BlockSpec(memory_space=VM)
        piece = shape((chips, depth, count * rows, width))
        keep, send = pl.pallas_call(
            functools.partial(split_kernel, count, chips, depth),
            name="split_grads",
            out_shape=(piece, piece),
            in_specs=[pl.BlockSpec(memory_space=pltpu.SMEM)] + [spec] * count,
            out_specs=(spec, spec),
        )(place_info(), *grads)
    else:
        pieces = jnp.stack(grads).reshape(count, 2 * chips, rows, depth, width)
        pieces = pieces.transpose(1, 3, 0, 2, 4).reshape(2 * chips, depth, count * rows, width)
        pieces = jnp.take(pieces, lax.axis_index("dp") ^ jnp.arange(chips * 2), axis=0)
        pieces = jnp.take(pieces, lax.axis_index("tensor") ^ jnp.arange(depth), axis=1)
        pieces = pieces.reshape((chips, 2) + pieces.shape[1:])
        keep, send = pieces[:, 0], pieces[:, 1]
    plane = add_low(keep, swap(send, "dp", 1)).astype(bf16)
    arrived = [swap(plane[a], "dp", a << 1) for a in range(1, chips)]
    column = add_low(plane[0], *arrived).astype(bf16)
    arrived = [swap(column[r], "tensor", r) for r in range(1, depth)]
    block = add_low(column[0], *arrived)
    return [block[i * rows : (i + 1) * rows] for i in range(count)]


def sum_everywhere(array):
    array = array + swap(array, "dp", 1)
    chips = lax.axis_size("dp") // 2
    array = add_low(array, *[swap(array, "dp", a << 1) for a in range(1, chips)])
    depth = lax.axis_size("tensor")
    return add_low(array, *[swap(array, "tensor", r) for r in range(1, depth)])


def on_device(
    inputs, memory, prefix,
    self_query, self_query_bias, self_key, self_value, self_value_bias, self_out, self_out_bias,
    self_norm_gain, self_norm_bias,
    cross_query, cross_query_bias, cross_key, cross_value, cross_value_bias, cross_out, cross_out_bias,
    cross_norm_gain, cross_norm_bias,
    feed_in, feed_in_bias, feed_out, feed_out_bias, feed_norm_gain, feed_norm_bias,
    cotangent,
):
    rows, width = inputs.shape
    depth = lax.axis_size("tensor")
    seqs = prefix.shape[0]
    assert rows * 2 == LEN and depth == 2 * seqs and memory.shape[0] * 2 == MEM
    pairs = width // LANES
    z = lax.axis_index("tensor")
    odd = z % 2
    prefix_here = jnp.where(odd == 1, 0, lax.dynamic_index_in_dim(prefix, z // 2, 0, keepdims=False))
    info = jnp.stack([prefix_here, odd]).astype(jnp.int32)

    x_oth = swap(inputs, "tensor", 1)
    wq, wk, wv = gather_weights([self_query, self_key, self_value])
    head_biases = jnp.concatenate(
        [b.astype(f32) for b in (self_query_bias, self_value_bias, cross_query_bias, cross_value_bias)]
        + [feed_in_bias.astype(f32)]
    )
    bias_all = lax.all_gather(head_biases, "tensor", axis=0, tiled=False)
    part = self_query_bias.shape[0]
    bq, bv, bcq, bcv = [
        bias_all[:, i * part : (i + 1) * part].reshape(1, depth * part) for i in range(4)
    ]
    bin_ = bias_all[:, 4 * part :].reshape(1, -1)
    mem_oth = swap(memory, "tensor", 1)
    wo, wcq, wck, wcv, wco = gather_weights(
        [self_out.T, cross_query, cross_key, cross_value, cross_out.T]
    )
    win, wout = gather_weights([feed_in, feed_out.T])

    def row(vector):
        return vector.astype(f32).reshape(1, -1)

    ff = win.shape[1]
    full = pl.BlockSpec((rows, width), lambda h: (0, 0))
    block = pl.BlockSpec((rows, LANES), lambda h: (0, h))
    wblock = pl.BlockSpec((width, LANES), lambda h: (0, h))
    bblock = pl.BlockSpec((1, LANES), lambda h: (0, h))
    eblock = pl.BlockSpec((2, rows, rows), lambda h: (h, 0, 0))
    lblock = pl.BlockSpec((1, rows, LANES), lambda h: (h, 0, 0))
    scalars = pl.BlockSpec(memory_space=pltpu.SMEM)
    square = shape((rows, width))
    heads = width // HD
    params = pltpu.CompilerParams(
        dimension_semantics=("arbitrary",), vmem_limit_bytes=60 * 2**20
    )
    q1, ko, kt, vo, vt, eo, et, ctx_one, linv_one = pl.pallas_call(
        self_forward_kernel,
        name="self_forward",
        grid=(pairs,),
        in_specs=[scalars, full, full, wblock, wblock, wblock, bblock, bblock],
        out_specs=(block, block, block, block, block, eblock, eblock, block, lblock),
        out_shape=(
            square, square, square, square, square,
            shape((heads, rows, rows)), shape((heads, rows, rows)), square,
            shape((pairs, rows, LANES), f32),
        ),
        compiler_params=params,
        cost_estimate=pl.CostEstimate(flops=12 * 10**9, transcendentals=0, bytes_accessed=2**24),
    )(info, inputs, x_oth, wq, wk, wv, bq, bv)

    fsquare = shape((rows, width), f32)
    thin = shape((rows, LANES), f32)
    mem_shape = shape((MEM, width))
    (n1, inv1, first_low, q2, k2, v2, e2, ctx_two, linv_two, n2, inv2) = whole_call(
        cross_forward_kernel, "cross_forward",
        [fsquare, thin, square, square, mem_shape, mem_shape, shape((heads, rows, MEM)), square,
         shape((pairs, rows, LANES), f32), fsquare, thin],
        [inputs, ctx_one, wo, row(self_out_bias), row(self_norm_gain), row(self_norm_bias), wcq, bcq,
         memory, mem_oth, wck, wcv, bcv, wco, row(cross_out_bias)],
        8 * 10**9,
    )
    vec8 = shape((8, width), f32)
    outputs, gout, gin, du2, vec_feed, vec_hidden = whole_call(
        feed_kernel, "feed",
        [square, shape((width, ff)), shape((width, ff)), fsquare, vec8, shape((1, ff), f32)],
        [n2, inv2, row(cross_norm_gain), row(cross_norm_bias), win, bin_, wout, row(feed_out_bias),
         row(feed_norm_gain), row(feed_norm_bias), cotangent],
        12 * 10**9,
        scratch=[VM((rows, ff), f32), VM((rows, ff), bf16), VM((rows, ff), bf16)],
    )
    grad_feed_in, grad_feed_out = scatter_weights([gin, gout])
    (gco, gcq, gck, gcv, gm_own, gm_oth, du1, dctx, go, vec_cross) = whole_call(
        cross_backward_kernel, "cross_backward",
        [square, square, square, square, shape(memory.shape, f32), shape(memory.shape), fsquare,
         square, square, vec8],
        [du2, wco, ctx_two, q2, k2, v2, e2, linv_two, first_low, memory, mem_oth, wcq, wck, wcv,
         n1, inv1, row(self_norm_gain), wo, ctx_one],
        12 * 10**9,
        scratch=[VM((rows, width), bf16), VM((rows, width), bf16), VM((MEM, width), bf16),
                 VM((MEM, width), bf16)],
    )
    grad_memory = gm_own + swap(gm_oth, "tensor", 1).astype(f32)
    grad_cross_out, grad_cross_query, grad_cross_key, grad_cross_value, grad_self_out = scatter_weights(
        [gco, gcq, gck, gcv, go]
    )
    dq, dko, dkt, dvo, dvt = pl.pallas_call(
        self_backward_kernel,
        name="self_backward",
        grid=(pairs,),
        in_specs=[scalars, block, block, block, block, block, eblock, eblock, block, lblock, block],
        out_specs=(block, block, block, block, block),
        out_shape=(square, square, square, square, square),
        compiler_params=params,
        cost_estimate=pl.CostEstimate(flops=16 * 10**9, transcendentals=0, bytes_accessed=2**24),
    )(info, q1, ko, kt, vo, vt, eo, et, ctx_one, linv_one, dctx)
    gq, gk, gv, gi_own, gi_oth, vec_self = whole_call(
        self_weights_kernel, "self_weights",
        [square, square, square, fsquare, square, vec8],
        [inputs, x_oth, dq, dko, dkt, dvo, dvt, wq, wk, wv, du1],
        4 * 10**9,
    )
    grad_inputs = gi_own + swap(gi_oth, "tensor", 1).astype(f32)
    grad_self_query, grad_self_key, grad_self_value = scatter_weights([gq, gk, gv])

    vectors = sum_everywhere(
        jnp.concatenate([vec_feed, vec_cross, vec_self, vec_hidden.reshape(-1, width)], axis=0)
    )

    def mine(vector):
        count = vector.shape[0] // depth
        return lax.dynamic_slice_in_dim(vector, z * count, count, 0)

    return (
        outputs,
        grad_inputs,
        grad_memory,
        grad_self_query,
        mine(vectors[16]),
        grad_self_key,
        grad_self_value,
        mine(vectors[17]),
        grad_self_out.T,
        vectors[12],
        vectors[10],
        vectors[11],
        grad_cross_query,
        mine(vectors[8]),
        grad_cross_key,
        grad_cross_value,
        mine(vectors[9]),
        grad_cross_out.T,
        vectors[5],
        vectors[3],
        vectors[4],
        grad_feed_in,
        mine(vectors[24:].reshape(-1)),
        grad_feed_out.T,
        vectors[2],
        vectors[0],
        vectors[1],
    )


ROWS = P(("dp", "tensor"), None)
GRID = P("dp", "tensor")
TURNED = P("tensor", "dp")
PART = P("tensor")
SAME = P()


def solution(mesh):
    attention = (GRID, PART, GRID, GRID, PART, TURNED, SAME, SAME, SAME)
    feed = (GRID, PART, TURNED, SAME, SAME, SAME)
    return jax.shard_map(
        on_device,
        mesh=mesh,
        in_specs=(ROWS, ROWS, P("dp")) + attention + attention + feed + (ROWS,),
        out_specs=(ROWS, ROWS, ROWS) + attention + attention + feed,
        check_vma=False,
    )
```
